256 devices in a mesh: expert: 8 (over z), tp: 8 (over x, core), dp: 4 (over y).
Axes of the slice: x: 4, y: 4, z: 8, core: 2. Of those that a mesh axis runs over, the one named last changes fastest.
Arguments:
- hidden: bfloat16 [1024, 6144], P(('expert', 'tp', 'dp')), may hold values from -400 to 400
- norm_gain: float32 [6144], replicated, may hold values from 0.1 to 1.9
- expert_ids: int32 [1024, 2], P(('expert', 'tp', 'dp')), may hold values from 0 to 7, all different within a row; in each aligned block of 4 rows (0 to 3, 4 to 7, ...) at most 2 rows name the same one
- router_logits: float32 [1024, 2], P(('expert', 'tp', 'dp')), may hold values from -6 to 6
- w_gate: bfloat16 [8, 6144, 8192], P('expert', None, ('tp', 'dp')), may hold values from -0.078125 to 0.078125
- w_up: bfloat16 [8, 6144, 8192], P('expert', None, ('tp', 'dp')), may hold values from -0.078125 to 0.078125
- w_down: bfloat16 [8, 8192, 6144], P('expert', ('tp', 'dp')), may hold values from -0.0625 to 0.0625
Outputs:
- moe_out: bfloat16 [1024, 6144], P(('expert', 'tp', 'dp'))
The draws below stay inside these ranges and needn't reach their ends.
Inputs may be any that keep to these rules, and one draw needn't show every extreme that they name: `expert_ids`: each token names two different experts; the tokens of one device name one expert at most 2 times.
All inputs are finite; a program needn't handle non-finite values.
Results may differ from the reference program's by a relative error of at most 0.015.
Values may be sent and summed in bfloat16 or wider, within the bound.
No kernel may reach another device: no remote copies, remote signals or barrier semaphores. Data moves between devices by JAX's collectives and lax.ppermute only.
A program may use at most 64 MiB of HBM per device.

```python
import math
import jax
import jax.numpy as jnp
import numpy as np
from jax import lax

D = 6144
FF = 8192
EXPERTS = 8
TOK_DEV = 4
MOST = 2
TOKENS = 1024
N_TP = 8
N_DP = 4


def draw_hidden(key, part):
    subkeys = jax.random.split(jax.random.fold_in(key, 11), 3)
    row_scale = jnp.exp(jax.random.uniform(subkeys[0], (TOKENS, 1), jnp.float32) * math.log(10.0))
    column_scale = jnp.exp(jax.random.uniform(subkeys[1], (1, D), jnp.float32) * math.log(10.0))
    values = jnp.clip(jax.random.normal(subkeys[2], (TOKENS, D), jnp.float32), -4.0, 4.0)
    return (values * row_scale * column_scale).astype(jnp.bfloat16)


def steps_of(stream_key, dims, pieces, low, largest):
    gain, own = 1.0, jax.random.fold_in(stream_key, 6)
    for dim, blocks in pieces:
        heights = jnp.exp(jax.random.uniform(jax.random.fold_in(own, dim), (blocks,), jnp.float32, low / len(pieces), largest / len(pieces)))
        gain = gain * jnp.repeat(heights, dims[dim] // blocks).reshape([-1 if axis == dim else 1 for axis in range(len(dims))])
    return gain


def shared_out(key, own, number, rows, count, top, bound, skew):
    sequence = jax.random.permutation(key, count)
    crowded, ordinary = portions_of(count, rows * top, bound, skew, True), portions_of(count, rows * top, bound, skew, False)
    places = jnp.arange(count)

    def named(tallies, offset_by):
        used = int((tallies > 0).sum())
        fixed = max(1, used // 4)
        shifted = fixed + (places - fixed + offset_by * (used - fixed)) % max(1, count - fixed)
        return jnp.zeros((count,), jnp.int32).at[sequence[jnp.where(places < fixed, places, shifted)]].set(jnp.asarray(tallies, jnp.int32))

    tallies = jnp.where(number % 4 == 0, named(crowded, number // 4), named(ordinary, number - number // 4 - 1))
    mixed = jax.random.permutation(jax.random.fold_in(own, 3), count)
    giver, sink = mixed[0:count // 2 * 2:2], mixed[1:count // 2 * 2:2]
    slack = jnp.minimum(tallies[giver] - 1, bound - tallies[sink]) // 2
    slack = jnp.where((giver == sequence[0]) | (sink == sequence[0]) | (tallies[sink] == 0), 0, jnp.maximum(slack, 0))
    shifted = jax.random.randint(jax.random.fold_in(own, 4), (count // 2,), 0, 1 << 20) % (slack + 1)
    tallies = tallies.at[giver].add(-shifted).at[sink].add(shifted)
    labels = jnp.searchsorted(jnp.cumsum(tallies), jnp.arange(rows * top), side="right").astype(jnp.int32)
    table = labels.reshape(top, rows).T
    table = table[jax.random.permutation(jax.random.fold_in(own, 1), rows)]
    offset_by = jax.random.randint(jax.random.fold_in(own, 2), (rows, 1), 0, top)
    return jnp.take_along_axis(table, (jnp.arange(top)[None, :] + offset_by) % top, axis=1)


def portions_of(number_of, total, most, skew, full):
    loads = [(1 << 20) // math.isqrt(rank ** skew) + 1 for rank in range(1, number_of + 1)]
    largest = most if full else min(most, max(-(-total // number_of), total * loads[0] // sum(loads)))
    least = 1 if total - largest >= number_of - 1 else 0
    holding, spare = [largest] + [least] * (number_of - 1), total - largest - least * (number_of - 1)
    while spare > 0:
        candidates = [i for i in range(1, number_of) if holding[i] < largest] or [i for i in range(1, number_of) if holding[i] < most]
        mass, left = sum([loads[i] for i in candidates]), spare
        for i in candidates:
            addition = min(most - holding[i], max(1, left * loads[i] // mass), spare)
            holding[i] = holding[i] + addition
            spare = spare - addition
    return np.array(holding)


def gaussian(stream_key, extent, deviation, bound, cuts=(), kind=jnp.bfloat16):
    drawn = deviation * jax.random.normal(stream_key, extent, jnp.float32)
    if cuts:
        drawn = drawn * steps_of(stream_key, extent, cuts, -0.22, 0.18)
    return jnp.clip(drawn, -bound, bound).astype(kind)


def setup_inputs(seed: int = 0) -> dict:
    seeds = jax.random.split(jax.random.key(seed), 8)
    hidden = draw_hidden(jax.random.fold_in(seeds[7], 71), 0)
    norm_gain = jnp.clip(1.0 + 0.18 * jax.random.normal(seeds[1], (D,), jnp.float32), 0.1, 1.9)
    expert_ids_keys = jax.random.split(jax.random.fold_in(seeds[2], 1), TOKENS // TOK_DEV)
    expert_ids_turns = jax.random.permutation(jax.random.fold_in(seeds[2], 3), TOKENS // TOK_DEV)
    expert_ids = jax.vmap(lambda own, number: shared_out(jax.random.fold_in(seeds[2], 2), own, number, TOK_DEV, EXPERTS, 2, MOST, 2))(expert_ids_keys, expert_ids_turns).reshape((TOKENS, 2))
    router_logits = gaussian(seeds[3], (TOKENS, 2), 1.5, 6.0, ((0, 256),), jnp.float32)
    w_gate = gaussian(seeds[4], (EXPERTS, D, FF), D ** -0.5, 0.078125, ((0, 8), (2, 32)))
    w_up = gaussian(seeds[5], (EXPERTS, D, FF), D ** -0.5, 0.078125, ((0, 8), (2, 32)))
    w_down = gaussian(seeds[6], (EXPERTS, FF, D), FF ** -0.5, 0.0625, ((0, 8), (1, 32)))
    return dict(hidden=hidden, norm_gain=norm_gain, expert_ids=expert_ids, router_logits=router_logits, w_gate=w_gate, w_up=w_up, w_down=w_down)


def slot_table(expert_ids):
    blocks = expert_ids.shape[0] // TOK_DEV
    assigned = expert_ids.reshape(blocks, TOK_DEV * 2)
    onehot = (assigned[:, :, None] == jnp.arange(EXPERTS, dtype=jnp.int32)[None, None, :]).astype(jnp.int32)
    earlier = jnp.cumsum(onehot, axis=1) - onehot
    position = lax.optimization_barrier(jnp.sum(earlier * onehot, axis=2)).astype(jnp.int32)
    chosen = assigned[:, None, None, :] == jnp.arange(EXPERTS, dtype=jnp.int32)[None, :, None, None]
    placed = position[:, None, None, :] == jnp.arange(MOST, dtype=jnp.int32)[None, None, :, None]
    return (chosen & placed).astype(jnp.float32)

def run_expert(operands):
    expert_rows, gate_mat, up_mat, down_mat = operands
    gate_val = jnp.dot(expert_rows, gate_mat, preferred_element_type=jnp.float32)
    up_val = jnp.dot(expert_rows, up_mat, preferred_element_type=jnp.float32)
    activation = (jax.nn.silu(gate_val) * up_val).astype(jnp.bfloat16)
    shares = N_TP * N_DP
    share_width = FF // shares

    def add_share(index, total):
        start = (index * share_width).astype(jnp.int32)
        act_part = lax.dynamic_slice_in_dim(activation, start, share_width, 1)
        down_part = lax.dynamic_slice_in_dim(down_mat, start, share_width, 0)
        part = jnp.dot(act_part, down_part, preferred_element_type=jnp.float32)
        rounded = lax.optimization_barrier(part.astype(jnp.bfloat16))
        return total + rounded.astype(jnp.float32)
    total = jnp.zeros((expert_rows.shape[0], down_mat.shape[1]), jnp.float32)
    total = lax.fori_loop(jnp.int32(0), jnp.int32(shares), add_share, total)
    return total.astype(jnp.bfloat16)

def reference(hidden, norm_gain, expert_ids, router_logits, w_gate, w_up, w_down):
    values = hidden.astype(jnp.float32)
    inverse = lax.rsqrt(lax.optimization_barrier(jnp.mean(values * values, axis=1, keepdims=True)) + 1e-05)
    normed = (values * inverse * norm_gain.astype(jnp.float32)[None, :]).astype(jnp.bfloat16)
    blocks = hidden.shape[0] // TOK_DEV
    selector = slot_table(expert_ids)
    repeated = jnp.repeat(normed, 2, axis=0).reshape(blocks, TOK_DEV * 2, D).astype(jnp.float32)
    bucketed = jnp.einsum('besa,bad->ebsd', selector, repeated).astype(jnp.bfloat16)
    bucketed = bucketed.reshape(EXPERTS, blocks * MOST, D)
    produced = lax.map(run_expert, (bucketed, w_gate, w_up, w_down))
    produced = produced.reshape(EXPERTS, blocks, MOST, D).astype(jnp.float32)
    picked = jnp.einsum('besa,ebsd->bad', selector, produced).reshape(hidden.shape[0], 2, D)
    first = jax.nn.sigmoid(router_logits[:, 0] - router_logits[:, 1])
    second = jax.nn.sigmoid(router_logits[:, 1] - router_logits[:, 0])
    route_weight = jnp.stack([first, second], axis=1).astype(jnp.float32)
    combined = lax.optimization_barrier(jnp.sum(picked * route_weight[:, :, None], axis=1))
    return combined.astype(jnp.bfloat16)
```

```python
import jax
import jax.numpy as jnp
from jax import lax
from jax.sharding import PartitionSpec as P

MOST = 2


def body(hidden, norm_gain, expert_ids, router_logits, w_gate, w_up, w_down):
    width = hidden.shape[1]
    values = hidden.astype(jnp.float32)
    inverse = lax.rsqrt(jnp.mean(values * values, axis=1, keepdims=True) + 1e-05)
    normed = (values * inverse * norm_gain[None, :]).astype(jnp.bfloat16)
    groups = lax.axis_size("expert")
    assigned = expert_ids.reshape(-1)
    onehot = (assigned[:, None] == jnp.arange(groups, dtype=jnp.int32)[None, :]).astype(jnp.int32)
    earlier = jnp.cumsum(onehot, axis=0) - onehot
    position = jnp.sum(earlier * onehot, axis=1)
    chosen = assigned[None, None, :] == jnp.arange(groups, dtype=jnp.int32)[:, None, None]
    placed = position[None, None, :] == jnp.arange(MOST, dtype=jnp.int32)[None, :, None]
    selector = (chosen & placed).astype(jnp.bfloat16).reshape(groups * MOST, assigned.shape[0])
    repeated = jnp.repeat(normed, 2, axis=0)
    bucket = jnp.dot(selector, repeated, preferred_element_type=jnp.float32).astype(jnp.bfloat16)
    arrived = lax.all_to_all(
        bucket.reshape(groups, MOST, width), "expert", split_axis=0, concat_axis=0, tiled=True
    )
    arrived = arrived.reshape(groups * MOST, width)
    gate_mat = w_gate[0]
    up_mat = w_up[0]
    down_mat = w_down[0]
    block_rows = lax.all_gather(arrived, ("tp", "dp"), axis=0, tiled=True)
    gate_val = jnp.dot(block_rows, gate_mat, preferred_element_type=jnp.float32)
    up_val = jnp.dot(block_rows, up_mat, preferred_element_type=jnp.float32)
    activations = (jax.nn.silu(gate_val) * up_val).astype(jnp.bfloat16)
    partial_sum = lax.psum_scatter(
        jnp.dot(activations, down_mat, preferred_element_type=jnp.float32).astype(jnp.bfloat16),
        ("tp", "dp"),
        scatter_dimension=0,
        tiled=True,
    )
    outgoing = partial_sum.reshape(groups, MOST, width)
    returned = lax.all_to_all(outgoing, "expert", split_axis=0, concat_axis=0, tiled=True)
    picked = jnp.dot(
        selector.T, returned.reshape(groups * MOST, width), preferred_element_type=jnp.float32
    )
    picked = picked.reshape(hidden.shape[0], 2, width)
    first = jax.nn.sigmoid(router_logits[:, 0] - router_logits[:, 1])
    second = jax.nn.sigmoid(router_logits[:, 1] - router_logits[:, 0])
    route_weight = jnp.stack([first, second], axis=1)
    combined = jnp.sum(picked * route_weight[:, :, None], axis=1)
    return combined.astype(jnp.bfloat16)


def solution(mesh):
    placed = (
        P(("expert", "tp", "dp"), None),
        P(),
        P(("expert", "tp", "dp"), None),
        P(("expert", "tp", "dp"), None),
        P("expert", None, ("tp", "dp")),
        P("expert", None, ("tp", "dp")),
        P("expert", ("tp", "dp"), None),
    )
    return jax.shard_map(
        body, mesh=mesh, in_specs=placed, out_specs=P(("expert", "tp", "dp"), None), check_vma=False
    )
```

```python
import jax
import jax.numpy as jnp
from jax import lax
from jax.sharding import PartitionSpec as P

MOST = 2
PLANE = ("tp", "dp")


def plane_pairs(n_tp, n_dp, step):
    n_x = n_tp // 2
    pairs = []
    for tp in range(n_tp):
        for y in range(n_dp):
            to_x, to_y, to_core = step(tp // 2, y, tp % 2)
            target = (to_x % n_x * 2 + to_core) * n_dp + to_y % n_dp
            pairs.append((tp * n_dp + y, target))
    return pairs


def first_ring(k):
    return lambda x, y, c: (x + k * c, y + k * (1 - c), c)


def second_ring(k):
    return lambda x, y, c: (x + k * (1 - c), y + k * c, c)


def body(hidden, norm_gain, expert_ids, router_logits, w_gate, w_up, w_down):
    width = hidden.shape[1]
    half = width // 2
    n_tp, n_dp = lax.axis_size("tp"), lax.axis_size("dp")
    core = lax.axis_index("tp") % 2
    low = core == 0

    def move(value, step):
        return lax.ppermute(value, PLANE, plane_pairs(n_tp, n_dp, step))

    def swap(value):
        return move(value, lambda x, y, c: (x, y, 1 - c))

    def own_half(value):
        return jnp.where(low, value[..., :half], value[..., half:])

    def other_half(value):
        return jnp.where(low, value[..., half:], value[..., :half])

    def joined(own, other):
        return jnp.where(
            low, jnp.concatenate([own, other], axis=-1), jnp.concatenate([other, own], axis=-1)
        )

    values = hidden.astype(jnp.float32)
    inverse = lax.rsqrt(jnp.mean(values * values, axis=1, keepdims=True) + 1e-05)
    normed = (values * inverse * norm_gain[None, :]).astype(jnp.bfloat16)
    groups = lax.axis_size("expert")
    assigned = expert_ids.reshape(-1)
    onehot = (assigned[:, None] == jnp.arange(groups, dtype=jnp.int32)[None, :]).astype(jnp.int32)
    earlier = jnp.cumsum(onehot, axis=0) - onehot
    position = jnp.sum(earlier * onehot, axis=1)
    chosen = assigned[None, None, :] == jnp.arange(groups, dtype=jnp.int32)[:, None, None]
    placed = position[None, None, :] == jnp.arange(MOST, dtype=jnp.int32)[None, :, None]
    selector = (chosen & placed).astype(jnp.bfloat16).reshape(groups * MOST, assigned.shape[0])
    repeated = jnp.repeat(normed, 2, axis=0)
    bucket = jnp.dot(selector, repeated, preferred_element_type=jnp.float32).astype(jnp.bfloat16)
    arrived = lax.all_to_all(
        bucket.reshape(groups, MOST, width), "expert", split_axis=0, concat_axis=0, tiled=True
    )
    arrived = arrived.reshape(groups * MOST, width)
    rows = groups * MOST

    mine = own_half(arrived)
    theirs = swap(other_half(arrived))
    pair = jnp.where(
        low, jnp.concatenate([mine, theirs], axis=0), jnp.concatenate([theirs, mine], axis=0)
    )
    line = jnp.concatenate(
        [
            pair,
            move(pair, first_ring(-1)),
            move(pair, first_ring(1)),
            move(pair, first_ring(2)),
        ],
        axis=0,
    )
    line_rows = line.shape[0]
    cut = line_rows // 2
    after = move(line, second_ring(-1))
    before = move(line, second_ring(1))
    far_top = move(before[:cut], second_ring(1))
    far_bottom = move(after[cut:], second_ring(-1))
    own_x = jnp.concatenate([line, after, before, far_top, far_bottom], axis=0)
    other_x = swap(own_x)

    def reordered(value):
        blocks = value.reshape(4, 4, 2 * rows, value.shape[-1])
        return jnp.swapaxes(blocks, 0, 1).reshape(value.shape)

    def weight_half(matrix, which):
        return lax.dynamic_slice_in_dim(matrix, which * half, half, 0)

    both = []
    for matrix in (w_gate[0], w_up[0]):
        own = jnp.dot(own_x, weight_half(matrix, core), preferred_element_type=jnp.float32)
        other = jnp.dot(
            other_x, weight_half(matrix, 1 - core), preferred_element_type=jnp.float32
        )
        both.append(own + reordered(other))
    activations = (jax.nn.silu(both[0]) * both[1]).astype(jnp.bfloat16)
    down_mat = w_down[0]

    def down(which):
        matrix = lax.dynamic_slice_in_dim(down_mat, which * half, half, 1)
        return jnp.dot(activations, matrix, preferred_element_type=jnp.float32)

    given = swap(down(1 - core).astype(jnp.bfloat16))
    total = down(core).astype(jnp.bfloat16).astype(jnp.float32) + reordered(given).astype(
        jnp.float32
    )
    total = total.astype(jnp.bfloat16).reshape(4, line_rows, half)
    kept, to_after, to_before, to_far = total[0], total[1], total[2], total[3]

    def add(*terms):
        result = terms[0].astype(jnp.float32)
        for term in terms[1:]:
            result = result + term.astype(jnp.float32)
        return result

    through_top = move(to_far[:cut], second_ring(1))
    through_bottom = move(to_far[cut:], second_ring(-1))
    to_after = jnp.concatenate(
        [add(to_after[:cut], through_top).astype(jnp.bfloat16), to_after[cut:]], axis=0
    )
    to_before = jnp.concatenate(
        [to_before[:cut], add(to_before[cut:], through_bottom).astype(jnp.bfloat16)], axis=0
    )
    line_sum = add(
        kept, move(to_after, second_ring(1)), move(to_before, second_ring(-1))
    ).astype(jnp.bfloat16)
    line_sum = line_sum.reshape(4, 2 * rows, half)
    pair_sum = add(
        line_sum[0],
        move(line_sum[1], first_ring(1)),
        move(line_sum[2], first_ring(-1)),
        move(line_sum[3], first_ring(2)),
    ).astype(jnp.bfloat16)
    mine = jnp.where(low, pair_sum[:rows], pair_sum[rows:])
    theirs = swap(jnp.where(low, pair_sum[rows:], pair_sum[:rows]))
    summed = joined(mine, theirs)

    outgoing = summed.reshape(groups, MOST, width)
    returned = lax.all_to_all(outgoing, "expert", split_axis=0, concat_axis=0, tiled=True)
    picked = jnp.dot(
        selector.T, returned.reshape(groups * MOST, width), preferred_element_type=jnp.float32
    )
    picked = picked.reshape(hidden.shape[0], 2, width)
    first = jax.nn.sigmoid(router_logits[:, 0] - router_logits[:, 1])
    second = jax.nn.sigmoid(router_logits[:, 1] - router_logits[:, 0])
    route_weight = jnp.stack([first, second], axis=1)
    combined = jnp.sum(picked * route_weight[:, :, None], axis=1)
    return combined.astype(jnp.bfloat16)


def solution(mesh):
    placed = (
        P(("expert", "tp", "dp"), None),
        P(),
        P(("expert", "tp", "dp"), None),
        P(("expert", "tp", "dp"), None),
        P("expert", None, ("tp", "dp")),
        P("expert", None, ("tp", "dp")),
        P("expert", ("tp", "dp"), None),
    )
    return jax.shard_map(
        body, mesh=mesh, in_specs=placed, out_specs=P(("expert", "tp", "dp"), None), check_vma=False
    )
```

```python
import jax
import jax.numpy as jnp
from jax import lax
from jax.sharding import PartitionSpec as P


MOST = 2
PLANE = ("tp", "dp")


def plane_pairs(n_tp, n_dp, step):
    n_x = n_tp // 2
    pairs = []
    for tp in range(n_tp):
        for y in range(n_dp):
            to_x, to_y, to_core = step(tp // 2, y, tp % 2)
            target = (to_x % n_x * 2 + to_core) * n_dp + to_y % n_dp
            pairs.append((tp * n_dp + y, target))
    return pairs


def first_ring(k):
    return lambda x, y, c: (x + k * c, y + k * (1 - c), c)


def second_ring(k):
    return lambda x, y, c: (x + k * (1 - c), y + k * c, c)


def layer(hidden, norm_gain, expert_ids, router_logits, w_gate, w_up, w_down):
    width = hidden.shape[1]
    half = width // 2
    n_tp, n_dp = lax.axis_size("tp"), lax.axis_size("dp")
    core = lax.axis_index("tp") % 2
    low = core == 0

    def move(value, step):
        return lax.ppermute(value, PLANE, plane_pairs(n_tp, n_dp, step))

    def swap(value):
        return move(value, lambda x, y, c: (x, y, 1 - c))

    def own_half(value):
        return jnp.where(low, value[..., :half], value[..., half:])

    def other_half(value):
        return jnp.where(low, value[..., half:], value[..., :half])

    def joined(own, other):
        return jnp.where(
            low, jnp.concatenate([own, other], axis=-1), jnp.concatenate([other, own], axis=-1)
        )

    values = hidden.astype(jnp.float32)
    inverse = lax.rsqrt(jnp.mean(values * values, axis=1, keepdims=True) + 1e-05)
    normed = (values * inverse * norm_gain[None, :]).astype(jnp.bfloat16)
    groups = lax.axis_size("expert")
    assigned = expert_ids.reshape(-1)
    onehot = (assigned[:, None] == jnp.arange(groups, dtype=jnp.int32)[None, :]).astype(jnp.int32)
    earlier = jnp.cumsum(onehot, axis=0) - onehot
    position = jnp.sum(earlier * onehot, axis=1)
    chosen = assigned[None, None, :] == jnp.arange(groups, dtype=jnp.int32)[:, None, None]
    placed = position[None, None, :] == jnp.arange(MOST, dtype=jnp.int32)[None, :, None]
    selector = (chosen & placed).astype(jnp.bfloat16).reshape(groups * MOST, assigned.shape[0])
    repeated = jnp.repeat(normed, 2, axis=0)
    bucket = jnp.dot(selector, repeated, preferred_element_type=jnp.float32).astype(jnp.bfloat16)
    arrived = lax.all_to_all(
        bucket.reshape(groups, MOST, width), "expert", split_axis=0, concat_axis=0, tiled=True
    )
    arrived = arrived.reshape(groups * MOST, width)
    rows = groups * MOST

    mine = own_half(arrived)
    theirs = swap(other_half(arrived))
    pair = jnp.where(
        low, jnp.concatenate([mine, theirs], axis=0), jnp.concatenate([theirs, mine], axis=0)
    )
    line = jnp.concatenate(
        [pair, move(pair, first_ring(-1)), move(pair, first_ring(1)), move(pair, first_ring(2))],
        axis=0,
    )
    line_rows = line.shape[0]
    cut = line_rows // 2
    ahead, back = second_ring(1), second_ring(-1)

    before_top = move(line[:cut], ahead)
    after_bottom = move(line[cut:], back)
    after_top = move(line[:cut], back)
    before_bottom = move(line[cut:], ahead)
    far_top = move(before_top, ahead)
    far_bottom = move(after_bottom, back)
    own_x = [
        line,
        jnp.concatenate([after_top, after_bottom], axis=0),
        jnp.concatenate([before_top, before_bottom], axis=0),
        jnp.concatenate([far_top, far_bottom], axis=0),
    ]
    other_x = [swap(block) for block in own_x]

    def reordered(value):
        blocks = value.reshape(4, 4, 2 * rows, value.shape[-1])
        return jnp.swapaxes(blocks, 0, 1).reshape(value.shape)

    def both_halves(matrix):
        own = lax.dynamic_slice_in_dim(matrix, core * half, half, 0)
        other = lax.dynamic_slice_in_dim(matrix, (1 - core) * half, half, 0)

        def product(block, part):
            return jnp.dot(block, part, preferred_element_type=jnp.float32)

        own = [product(own_x[i], own) for i in range(4)]
        other = [product(other_x[i], other) for i in range(4)]
        return jnp.concatenate(own, axis=0) + reordered(jnp.concatenate(other, axis=0))

    gate_val, up_val = both_halves(w_gate[0]), both_halves(w_up[0])
    activations = (jax.nn.silu(gate_val) * up_val).astype(jnp.bfloat16)
    for_partner = reordered(activations).reshape(4, line_rows, -1)
    activations = activations.reshape(4, line_rows, -1)
    down_own = lax.dynamic_slice_in_dim(w_down[0], core * half, half, 1)
    down_other = lax.dynamic_slice_in_dim(w_down[0], (1 - core) * half, half, 1)

    def add(*terms):
        result = terms[0].astype(jnp.float32)
        for term in terms[1:]:
            result = result + term.astype(jnp.float32)
        return result

    def down(block):
        given = jnp.dot(for_partner[block], down_other, preferred_element_type=jnp.float32)
        given = swap(given.astype(jnp.bfloat16))
        kept = jnp.dot(activations[block], down_own, preferred_element_type=jnp.float32)
        return add(kept.astype(jnp.bfloat16), given)

    low_type = jnp.bfloat16
    to_far = down(3).astype(low_type)
    through_top = move(to_far[:cut], ahead)
    through_bottom = move(to_far[cut:], back)
    to_after = down(1)
    to_before = down(2)
    from_before_bottom = move(to_after[cut:].astype(low_type), ahead)
    from_after_top = move(to_before[:cut].astype(low_type), back)
    from_before_top = move(add(to_after[:cut], through_top).astype(low_type), ahead)
    from_after_bottom = move(add(to_before[cut:], through_bottom).astype(low_type), back)
    kept = down(0)
    line_sum = jnp.concatenate(
        [
            add(kept[:cut], from_before_top, from_after_top),
            add(kept[cut:], from_before_bottom, from_after_bottom),
        ],
        axis=0,
    ).astype(low_type)
    line_sum = line_sum.reshape(4, 2 * rows, half)
    pair_sum = add(
        line_sum[0],
        move(line_sum[1], first_ring(1)),
        move(line_sum[2], first_ring(-1)),
        move(line_sum[3], first_ring(2)),
    ).astype(jnp.bfloat16)
    mine = jnp.where(low, pair_sum[:rows], pair_sum[rows:])
    theirs = swap(jnp.where(low, pair_sum[rows:], pair_sum[:rows]))
    summed = joined(mine, theirs)

    outgoing = summed.reshape(groups, MOST, width)
    returned = lax.all_to_all(outgoing, "expert", split_axis=0, concat_axis=0, tiled=True)
    picked = jnp.dot(
        selector.T, returned.reshape(groups * MOST, width), preferred_element_type=jnp.float32
    )
    picked = picked.reshape(hidden.shape[0], 2, width)
    first = jax.nn.sigmoid(router_logits[:, 0] - router_logits[:, 1])
    second = jax.nn.sigmoid(router_logits[:, 1] - router_logits[:, 0])
    route_weight = jnp.stack([first, second], axis=1)
    combined = jnp.sum(picked * route_weight[:, :, None], axis=1)
    return combined.astype(jnp.bfloat16)


def solution(mesh):
    placed = (
        P(("expert", "tp", "dp"), None),
        P(),
        P(("expert", "tp", "dp"), None),
        P(("expert", "tp", "dp"), None),
        P("expert", None, ("tp", "dp")),
        P("expert", None, ("tp", "dp")),
        P("expert", ("tp", "dp"), None),
    )
    return jax.shard_map(
        layer, mesh=mesh, in_specs=placed, out_specs=P(("expert", "tp", "dp"), None), check_vma=False
    )
```

```python
import jax
import jax.numpy as jnp
from jax import lax
from jax.sharding import PartitionSpec as P


MOST = 2
PLANE = ("tp", "dp")


def plane_pairs(n_tp, n_dp, step):
    n_x = n_tp // 2
    pairs = []
    for tp in range(n_tp):
        for y in range(n_dp):
            to_x, to_y, to_core = step(tp // 2, y, tp % 2)
            target = (to_x % n_x * 2 + to_core) * n_dp + to_y % n_dp
            pairs.append((tp * n_dp + y, target))
    return pairs


def first_ring(k):
    return lambda x, y, c: (x + k * c, y + k * (1 - c), c)


def second_ring(k):
    return lambda x, y, c: (x + k * (1 - c), y + k * c, c)


def layer(hidden, norm_gain, expert_ids, router_logits, w_gate, w_up, w_down):
    width = hidden.shape[1]
    half = width // 2
    n_tp, n_dp = lax.axis_size("tp"), lax.axis_size("dp")
    core = lax.axis_index("tp") % 2
    low = core == 0

    def move(value, step):
        return lax.ppermute(value, PLANE, plane_pairs(n_tp, n_dp, step))

    def swap(value):
        return move(value, lambda x, y, c: (x, y, 1 - c))

    def own_half(value):
        return jnp.where(low, value[..., :half], value[..., half:])

    def other_half(value):
        return jnp.where(low, value[..., half:], value[..., :half])

    def joined(own, other):
        return jnp.where(
            low, jnp.concatenate([own, other], axis=-1), jnp.concatenate([other, own], axis=-1)
        )

    values = hidden.astype(jnp.float32)
    inverse = lax.rsqrt(jnp.mean(values * values, axis=1, keepdims=True) + 1e-05)
    normed = (values * inverse * norm_gain[None, :]).astype(jnp.bfloat16)
    groups = lax.axis_size("expert")
    assigned = expert_ids.reshape(-1)
    onehot = (assigned[:, None] == jnp.arange(groups, dtype=jnp.int32)[None, :]).astype(jnp.int32)
    earlier = jnp.cumsum(onehot, axis=0) - onehot
    position = jnp.sum(earlier * onehot, axis=1)
    chosen = assigned[None, None, :] == jnp.arange(groups, dtype=jnp.int32)[:, None, None]
    placed = position[None, None, :] == jnp.arange(MOST, dtype=jnp.int32)[None, :, None]
    selector = (chosen & placed).astype(jnp.bfloat16).reshape(groups * MOST, assigned.shape[0])
    repeated = jnp.repeat(normed, 2, axis=0)
    bucket = jnp.dot(selector, repeated, preferred_element_type=jnp.float32).astype(jnp.bfloat16)
    arrived = lax.all_to_all(
        bucket.reshape(groups, MOST, width), "expert", split_axis=0, concat_axis=0, tiled=True
    )
    arrived = arrived.reshape(groups * MOST, width)
    rows = groups * MOST

    mine = own_half(arrived)
    theirs = swap(other_half(arrived))
    pair = jnp.where(
        low, jnp.concatenate([mine, theirs], axis=0), jnp.concatenate([theirs, mine], axis=0)
    )

    def stacked(*parts):
        total = jnp.zeros((sum(part.shape[0] for part in parts), half), jnp.bfloat16)
        at = 0
        for part in parts:
            total = lax.dynamic_update_slice(total, part, (at, 0))
            at += part.shape[0]
        return total

    in_after = move(pair, first_ring(-1))
    in_before = move(pair, first_ring(1))
    in_far = move(pair, first_ring(2))
    top, bottom = stacked(pair, in_after), stacked(in_before, in_far)
    line = lax.optimization_barrier(stacked(pair, in_after, in_before, in_far))
    line_rows = line.shape[0]
    cut = line_rows // 2
    ahead, back = second_ring(1), second_ring(-1)

    before_top = move(top, ahead)
    after_bottom = move(bottom, back)
    after_top = move(top, back)
    before_bottom = move(bottom, ahead)
    far_top = move(before_top, ahead)
    far_bottom = move(after_bottom, back)
    own_x = [
        line,
        jnp.concatenate([after_top, after_bottom], axis=0),
        jnp.concatenate([before_top, before_bottom], axis=0),
        jnp.concatenate([far_top, far_bottom], axis=0),
    ]
    other_x = [swap(block) for block in own_x]

    seat = 2 * rows

    def both_halves(matrix, kind):
        own = lax.dynamic_slice_in_dim(matrix, core * half, half, 0)
        other = lax.dynamic_slice_in_dim(matrix, (1 - core) * half, half, 0)

        def product(block, part):
            return lax.optimization_barrier(
                jnp.dot(block, part, preferred_element_type=jnp.float32)
            )

        own = [
            product(own_x[0], own),
            product(own_x[1], own),
            jnp.concatenate(
                [product(before_top, own), product(before_bottom, own)],
                axis=0,
            )
            if kind == "g"
            else product(own_x[2], own),
            product(own_x[3], own),
        ]
        other = [product(other_x[i], other) for i in range(4)]
        return [
            own[i]
            + jnp.concatenate([part[i * seat : (i + 1) * seat] for part in other], axis=0)
            for i in range(4)
        ]

    gate_val, up_val = both_halves(w_gate[0], "g"), both_halves(w_up[0], "u")
    activations = [
        (jax.nn.silu(gate) * up).astype(jnp.bfloat16) for gate, up in zip(gate_val, up_val)
    ]
    for_partner = [
        jnp.concatenate([part[i * seat : (i + 1) * seat] for part in activations], axis=0)
        for i in range(4)
    ]
    down_own = lax.dynamic_slice_in_dim(w_down[0], core * half, half, 1)
    down_other = lax.dynamic_slice_in_dim(w_down[0], (1 - core) * half, half, 1)

    def add(*terms):
        result = terms[0].astype(jnp.float32)
        for term in terms[1:]:
            result = result + term.astype(jnp.float32)
        return result

    def down(block):
        given = jnp.dot(for_partner[block], down_other, preferred_element_type=jnp.float32)
        given = swap(given.astype(jnp.bfloat16))
        kept = jnp.dot(activations[block], down_own, preferred_element_type=jnp.float32)
        return add(kept.astype(jnp.bfloat16), given)

    low_type = jnp.bfloat16
    to_far = down(3).astype(low_type)
    through_top = move(to_far[:cut], ahead)
    through_bottom = move(to_far[cut:], back)
    to_after = down(1)
    to_before = down(2)
    from_before_bottom = move(to_after[cut:].astype(low_type), ahead)
    from_after_top = move(to_before[:cut].astype(low_type), back)
    from_before_top = move(add(to_after[:cut], through_top).astype(low_type), ahead)
    from_after_bottom = move(add(to_before[cut:], through_bottom).astype(low_type), back)
    kept = down(0)
    line_sum = jnp.concatenate(
        [
            add(kept[:cut], from_before_top, from_after_top),
            add(kept[cut:], from_before_bottom, from_after_bottom),
        ],
        axis=0,
    ).astype(low_type)
    line_sum = line_sum.reshape(4, 2 * rows, half)
    pair_sum = add(
        line_sum[0],
        move(line_sum[1], first_ring(1)),
        move(line_sum[2], first_ring(-1)),
        move(line_sum[3], first_ring(2)),
    ).astype(jnp.bfloat16)
    mine = jnp.where(low, pair_sum[:rows], pair_sum[rows:])
    theirs = swap(jnp.where(low, pair_sum[rows:], pair_sum[:rows]))
    summed = joined(mine, theirs)

    outgoing = summed.reshape(groups, MOST, width)
    returned = lax.all_to_all(outgoing, "expert", split_axis=0, concat_axis=0, tiled=True)
    picked = jnp.dot(
        selector.T, returned.reshape(groups * MOST, width), preferred_element_type=jnp.float32
    )
    picked = picked.reshape(hidden.shape[0], 2, width)
    first = jax.nn.sigmoid(router_logits[:, 0] - router_logits[:, 1])
    second = jax.nn.sigmoid(router_logits[:, 1] - router_logits[:, 0])
    route_weight = jnp.stack([first, second], axis=1)
    combined = jnp.sum(picked * route_weight[:, :, None], axis=1)
    return combined.astype(jnp.bfloat16)


def solution(mesh):
    placed = (
        P(("expert", "tp", "dp"), None),
        P(),
        P(("expert", "tp", "dp"), None),
        P(("expert", "tp", "dp"), None),
        P("expert", None, ("tp", "dp")),
        P("expert", None, ("tp", "dp")),
        P("expert", ("tp", "dp"), None),
    )
    return jax.shard_map(
        layer, mesh=mesh, in_specs=placed, out_specs=P(("expert", "tp", "dp"), None), check_vma=False
    )
```

```python
import jax
import jax.numpy as jnp
from jax import lax
from jax.sharding import PartitionSpec as P


MOST = 2
PLANE = ("tp", "dp")


def plane_pairs(n_tp, n_dp, step):
    n_x = n_tp // 2
    pairs = []
    for tp in range(n_tp):
        for y in range(n_dp):
            to_x, to_y, to_core = step(tp // 2, y, tp % 2)
            target = (to_x % n_x * 2 + to_core) * n_dp + to_y % n_dp
            pairs.append((tp * n_dp + y, target))
    return pairs


def first_ring(k):
    return lambda x, y, c: (x + k * c, y + k * (1 - c), c)


def second_ring(k):
    return lambda x, y, c: (x + k * (1 - c), y + k * c, c)


def layer(hidden, norm_gain, expert_ids, router_logits, w_gate, w_up, w_down):
    width = hidden.shape[1]
    half = width // 2
    n_tp, n_dp = lax.axis_size("tp"), lax.axis_size("dp")
    core = lax.axis_index("tp") % 2
    low = core == 0

    def move(value, step):
        return lax.ppermute(value, PLANE, plane_pairs(n_tp, n_dp, step))

    def swap(value):
        return move(value, lambda x, y, c: (x, y, 1 - c))

    def own_half(value):
        return jnp.where(low, value[..., :half], value[..., half:])

    def other_half(value):
        return jnp.where(low, value[..., half:], value[..., :half])

    def joined(own, other):
        return jnp.where(
            low, jnp.concatenate([own, other], axis=-1), jnp.concatenate([other, own], axis=-1)
        )

    values = hidden.astype(jnp.float32)
    inverse = lax.rsqrt(jnp.mean(values * values, axis=1, keepdims=True) + 1e-05)
    normed = (values * inverse * norm_gain[None, :]).astype(jnp.bfloat16)
    groups = lax.axis_size("expert")
    assigned = expert_ids.reshape(-1)
    onehot = (assigned[:, None] == jnp.arange(groups, dtype=jnp.int32)[None, :]).astype(jnp.int32)
    earlier = jnp.cumsum(onehot, axis=0) - onehot
    position = jnp.sum(earlier * onehot, axis=1)
    chosen = assigned[None, None, :] == jnp.arange(groups, dtype=jnp.int32)[:, None, None]
    placed = position[None, None, :] == jnp.arange(MOST, dtype=jnp.int32)[None, :, None]
    selector = (chosen & placed).astype(jnp.bfloat16).reshape(groups * MOST, assigned.shape[0])
    repeated = jnp.repeat(normed, 2, axis=0)
    bucket = jnp.dot(selector, repeated, preferred_element_type=jnp.float32).astype(jnp.bfloat16)
    arrived = lax.all_to_all(
        bucket.reshape(groups, MOST, width), "expert", split_axis=0, concat_axis=0, tiled=True
    )
    arrived = arrived.reshape(groups * MOST, width)
    rows = groups * MOST

    mine = own_half(arrived)
    theirs = swap(other_half(arrived))
    pair = jnp.where(
        low, jnp.concatenate([mine, theirs], axis=0), jnp.concatenate([theirs, mine], axis=0)
    )

    def stacked(*parts):
        total = jnp.zeros((sum(part.shape[0] for part in parts), half), jnp.bfloat16)
        at = 0
        for part in parts:
            total = lax.dynamic_update_slice(total, part, (at, 0))
            at += part.shape[0]
        return total

    in_after = move(pair, first_ring(-1))
    in_before = move(pair, first_ring(1))
    in_far = move(pair, first_ring(2))
    top, bottom = stacked(pair, in_after), stacked(in_before, in_far)
    line = lax.optimization_barrier(stacked(pair, in_after, in_before, in_far))
    line_rows = line.shape[0]
    cut = line_rows // 2
    ahead, back = second_ring(1), second_ring(-1)

    before_top = move(top, ahead)
    after_bottom = move(bottom, back)
    after_top = move(top, back)
    before_bottom = move(bottom, ahead)
    far_top = move(before_top, ahead)
    far_bottom = move(after_bottom, back)
    own_x = [
        line,
        jnp.concatenate([after_top, after_bottom], axis=0),
        jnp.concatenate([before_top, before_bottom], axis=0),
        jnp.concatenate([far_top, far_bottom], axis=0),
    ]
    other_x = [swap(block) for block in own_x]

    seat = 2 * rows

    def both_halves(matrix, kind):
        own = lax.dynamic_slice_in_dim(matrix, core * half, half, 0)
        other = lax.dynamic_slice_in_dim(matrix, (1 - core) * half, half, 0)

        def product(block, part):
            return lax.optimization_barrier(
                jnp.dot(block, part, preferred_element_type=jnp.float32)
            )

        own = [
            product(own_x[0], own),
            product(own_x[1], own),
            jnp.concatenate(
                [product(before_top, own), product(before_bottom, own)],
                axis=0,
            )
            if kind == "g"
            else product(own_x[2], own),
            product(own_x[3], own),
        ]
        other = [product(other_x[i], other) for i in range(4)]
        return [
            own[i]
            + jnp.concatenate([part[i * seat : (i + 1) * seat] for part in other], axis=0)
            for i in range(4)
        ]

    gate_val, up_val = both_halves(w_gate[0], "g"), both_halves(w_up[0], "u")
    activations = [
        (jax.nn.silu(gate) * up).astype(jnp.bfloat16) for gate, up in zip(gate_val, up_val)
    ]
    for_partner = [
        jnp.concatenate([part[i * seat : (i + 1) * seat] for part in activations], axis=0)
        for i in range(4)
    ]
    down_own = lax.dynamic_slice_in_dim(w_down[0], core * half, half, 1)
    down_other = lax.dynamic_slice_in_dim(w_down[0], (1 - core) * half, half, 1)

    def add(*terms):
        result = terms[0].astype(jnp.float32)
        for term in terms[1:]:
            result = result + term.astype(jnp.float32)
        return result

    def down(block):
        given = jnp.dot(for_partner[block], down_other, preferred_element_type=jnp.float32)
        given = swap(given.astype(jnp.bfloat16))
        kept = jnp.dot(activations[block], down_own, preferred_element_type=jnp.float32)
        return add(kept.astype(jnp.bfloat16), given)

    low_type = jnp.bfloat16
    to_far = down(3).astype(low_type)
    through_top = move(to_far[:cut], ahead)
    through_bottom = move(to_far[cut:], back)
    to_after = down(1)
    to_before = down(2)
    from_before_bottom = move(to_after[cut:].astype(low_type), ahead)
    from_after_top = move(to_before[:cut].astype(low_type), back)
    from_before_top = move(add(to_after[:cut], through_top).astype(low_type), ahead)
    from_after_bottom = move(add(to_before[cut:], through_bottom).astype(low_type), back)
    kept = down(0)
    line_sum = jnp.concatenate(
        [
            add(kept[:cut], from_before_top, from_after_top),
            add(kept[cut:], from_before_bottom, from_after_bottom),
        ],
        axis=0,
    ).astype(low_type)
    line_sum = line_sum.reshape(4, 2 * rows, half)
    pair_sum = add(
        line_sum[0],
        move(line_sum[1], first_ring(1)),
        move(line_sum[2], first_ring(-1)),
        move(line_sum[3], first_ring(2)),
    ).astype(jnp.bfloat16)
    mine = jnp.where(low, pair_sum[:rows], pair_sum[rows:])
    theirs = swap(jnp.where(low, pair_sum[rows:], pair_sum[:rows]))
    outgoing = jnp.concatenate(
        [mine.reshape(groups, MOST, half), theirs.reshape(groups, MOST, half)], axis=1
    )
    returned = lax.all_to_all(outgoing, "expert", split_axis=0, concat_axis=0, tiled=True)
    parts = [
        jnp.dot(selector.T, part.reshape(rows, half), preferred_element_type=jnp.float32)
        for part in (returned[:, :MOST], returned[:, MOST:])
    ]
    picked = joined(*parts).reshape(hidden.shape[0], 2, width)
    first = jax.nn.sigmoid(router_logits[:, 0] - router_logits[:, 1])
    second = jax.nn.sigmoid(router_logits[:, 1] - router_logits[:, 0])
    route_weight = jnp.stack([first, second], axis=1)
    combined = jnp.sum(picked * route_weight[:, :, None], axis=1)
    return combined.astype(jnp.bfloat16)


def solution(mesh):
    placed = (
        P(("expert", "tp", "dp"), None),
        P(),
        P(("expert", "tp", "dp"), None),
        P(("expert", "tp", "dp"), None),
        P("expert", None, ("tp", "dp")),
        P("expert", None, ("tp", "dp")),
        P("expert", ("tp", "dp"), None),
    )
    return jax.shard_map(
        layer, mesh=mesh, in_specs=placed, out_specs=P(("expert", "tp", "dp"), None), check_vma=False
    )
```
